32 devices in a mesh: row: 4 (over z), col: 4 (over y, x), agent: 2 (over core).
Axes of the slice: x: 2, y: 2, z: 4, core: 2. Of those that a mesh axis runs over, the one named last changes fastest.
Arguments:
- raster: bfloat16 [2, 512, 512, 128], P(None, 'row', ('col', 'agent')), may hold values from -6 to 6
- first_kernel: bfloat16 [3, 3, 128, 128], replicated, may hold values from -0.1875 to 0.1875
- first_bias: float32 [128], replicated, may hold values from -3 to 3
- second_kernel: bfloat16 [3, 3, 128, 128], replicated, may hold values from -0.1875 to 0.1875
- second_bias: float32 [128], replicated, may hold values from -3 to 3
- queries: bfloat16 [256, 128], P('agent'), may hold values from -64 to 64
- agent_slot: int32 [256], replicated, may hold values from 0 to 255, each once
- regions: int32 [256, 4], replicated, may hold values from 0 to 8, as said below
Outputs:
- log_heatmap: float32 [2, 512, 512, 256], P(None, 'row', ('col', 'agent'))
The draws below stay inside these ranges and needn't reach their ends.
Inputs may be any that keep to these rules, and one draw needn't show every extreme that they name: regions[a,0] < regions[a,1] <= 8 and regions[a,2] < regions[a,3] <= 8.
All inputs are finite; a program needn't handle non-finite values.
Results may differ from the reference program's by a relative error of at most 0.0024.
Values may be sent and summed in bfloat16 or wider, within the bound.
A program may use at most 192 MiB of HBM per device.

```python
import jax
import jax.numpy as jnp

C = 128
A = 256
BLOCK = 64
SCENES = 2
H = 512
W = 512


def draw_queries(key, part):
    key_base = jax.random.fold_in(key, 11)
    key_pick = jax.random.fold_in(key, 14)
    key_jitter = jax.random.fold_in(key, 15)
    values = jnp.clip(0.4 * jax.random.normal(key_base, (A, C), jnp.float32), -1.6, 1.6)
    order = jax.random.permutation(key_pick, A)
    levels = jnp.zeros((A,), jnp.float32)
    levels = levels.at[order[0]].set(200.0 / C)
    levels = levels.at[order[1]].set(400.0 / C)
    levels = levels.at[order[2]].set(800.0 / C)
    jitter = 1.0 + 0.1 * jax.random.uniform(key_jitter, (A, C), jnp.float32, -1.0, 1.0)
    aligned = jnp.clip(levels[:, None] * jitter, -64.0, 64.0)
    values = jnp.where(levels[:, None] > 0.0, aligned, values)
    return values.astype(jnp.bfloat16)


def draw_regions(key, part):
    row_blocks = H // BLOCK
    col_blocks = W // BLOCK
    keys = [jax.random.fold_in(key, 21 + offset) for offset in range(4)]
    row_first = jax.random.randint(keys[0], (A,), 0, row_blocks // 2)
    row_end = row_first + jax.random.randint(keys[1], (A,), 1, row_blocks // 2 + 1)
    col_first = jax.random.randint(keys[2], (A,), 0, col_blocks // 2)
    col_end = col_first + jax.random.randint(keys[3], (A,), 1, col_blocks // 2 + 1)
    row_first = row_first.at[0].set(0)
    row_end = row_end.at[0].set(row_blocks)
    col_first = col_first.at[0].set(0)
    col_end = col_end.at[0].set(col_blocks)
    return jnp.stack([row_first, row_end, col_first, col_end], axis=1).astype(jnp.int32)


def level_of(stream_key, dims, pieces, smallest, largest):
    factor_of, own = 1.0, jax.random.fold_in(stream_key, 6)
    for dim, parts in pieces:
        steps = jnp.exp(jax.random.uniform(jax.random.fold_in(own, dim), (parts,), jnp.float32, smallest / len(pieces), largest / len(pieces)))
        factor_of = factor_of * jnp.repeat(steps, dims[dim] // parts).reshape([-1 if axis == dim else 1 for axis in range(len(dims))])
    return factor_of


def normal_values(stream_key, dims, spread, bound, split=(), held_as=jnp.bfloat16):
    drawn = spread * jax.random.normal(stream_key, dims, jnp.float32)
    if split:
        drawn = drawn * level_of(stream_key, dims, split, -0.22, 0.18)
    return jnp.clip(drawn, -bound, bound).astype(held_as)


def setup_inputs(seed: int = 0) -> dict:
    arg_keys = jax.random.split(jax.random.key(seed), 9)
    raster = normal_values(arg_keys[0], (SCENES, H, W, C), 1.0, 6.0, ((1, 4), (2, 8)))
    first_kernel = normal_values(arg_keys[1], (3, 3, C, C), (9 * C) ** -0.5, 0.1875)
    first_bias = normal_values(arg_keys[2], (C,), 0.5, 3.0, (), jnp.float32)
    second_kernel = normal_values(arg_keys[3], (3, 3, C, C), (9 * C) ** -0.5, 0.1875)
    second_bias = normal_values(arg_keys[4], (C,), 0.5, 3.0, (), jnp.float32)
    queries = draw_queries(jax.random.fold_in(arg_keys[8], 71), 0)
    agent_slot = jax.random.permutation(arg_keys[6], A).astype(jnp.int32)
    regions = draw_regions(jax.random.fold_in(arg_keys[8], 71), 0)
    return dict(raster=raster, first_kernel=first_kernel, first_bias=first_bias, second_kernel=second_kernel, second_bias=second_bias, queries=queries, agent_slot=agent_slot, regions=regions)


def dilated(image, kernel, bias, dilation):
    rows, cols, channels = image.shape
    padded = jnp.pad(image, ((dilation, dilation), (dilation, dilation), (0, 0)))
    running = jnp.zeros((rows * cols, kernel.shape[3]), jnp.float32)
    for row_tap in range(3):
        for col_tap in range(3):
            tap_piece = padded[row_tap * dilation:row_tap * dilation + rows, col_tap * dilation:col_tap * dilation + cols, :]
            running = running + jnp.dot(tap_piece.reshape(rows * cols, channels), kernel[row_tap, col_tap], preferred_element_type=jnp.float32)
    return jnp.maximum(running + bias, 0.0).astype(jnp.bfloat16).reshape(rows, cols, -1)


def reference(raster, first_kernel, first_bias, second_kernel, second_bias, queries, agent_slot, regions):
    ordered = queries[agent_slot]
    block_rows = jnp.arange(H, dtype=jnp.int32) // BLOCK
    block_cols = jnp.arange(W, dtype=jnp.int32) // BLOCK
    row_ok = (block_rows[:, None] >= regions[None, :, 0]) & (block_rows[:, None] < regions[None, :, 1])
    col_ok = (block_cols[:, None] >= regions[None, :, 2]) & (block_cols[:, None] < regions[None, :, 3])
    valid = row_ok[:, None, :] & col_ok[None, :, :]
    results = []
    for scene in range(SCENES):
        layer_one = dilated(raster[scene], first_kernel, first_bias, 4)
        layer_two = dilated(layer_one, second_kernel, second_bias, 8)
        logits = jnp.dot(layer_two.reshape(H * W, C), ordered.T, preferred_element_type=jnp.float32).reshape(H, W, A)
        masked = jnp.where(valid, logits, -1e30)
        peak = jnp.max(masked, axis=(0, 1))
        mass = jnp.sum(jnp.where(valid, jnp.exp(logits - peak), 0.0), axis=(0, 1))
        results.append(logits - (peak + jnp.log(mass)))
    return jnp.stack(results)
```

```python
import functools

import jax
import jax.numpy as jnp
from jax import lax
from jax.experimental import pallas as pl
from jax.experimental.pallas import tpu as pltpu
from jax.sharding import PartitionSpec as P

BLOCK = 64
PAD = 16
NEG = -1e30
MESH = pl.DeviceIdType.MESH
DIRS = ((-1, 0), (1, 0), (0, -1), (0, 1), (-1, -1), (-1, 1), (1, -1), (1, 1))
BF16 = jnp.bfloat16
F32 = jnp.float32


def field_kernel(
    nr, nc, na, scenes, rows, cols, agents,
    raster, w1, b1, w2, b2, queries, slot, regions,
    l2_out, keys_out, norm_out,
    xp1, xp2, l2, p_edge, p_land, q_edge, q_land, big1, big2, everyone,
    mine, got_q, got_r,
    load_sem, out_sem, h_send, h_recv, k_send, k_recv, sq_send, sq_recv, sr_send, sr_recv,
):
    r = lax.axis_index("row")
    c = lax.axis_index("col")
    a = lax.axis_index("agent")
    nq = nc * na
    q = c * na + a
    pairs = rows // 2
    ch = w1.shape[-1]

    def place(rr, qq):
        return {"row": rr, "col": qq // na, "agent": qq % na}

    def exists(rr, qq):
        return (rr >= 0) & (rr < nr) & (qq >= 0) & (qq < nq)

    barrier = pltpu.get_barrier_semaphore()
    for d in range(1, nr):
        pl.semaphore_signal(barrier, inc=1, device_id=place((r + d) % nr, q), device_id_type=MESH)
    for d in range(1, nq):
        pl.semaphore_signal(barrier, inc=1, device_id=place(r, (q + d) % nq), device_id_type=MESH)
    for dr, dq in DIRS[4:]:
        @pl.when(exists(r + dr, q + dq))
        def _(dr=dr, dq=dq):
            pl.semaphore_signal(barrier, inc=1, device_id=place(r + dr, q + dq), device_id_type=MESH)

    loads = [
        pltpu.make_async_copy(
            raster.at[s], xp1.at[s, pl.ds(2, pairs), :, pl.ds(PAD, cols), :], load_sem.at[s]
        )
        for s in range(scenes)
    ]
    for load in loads:
        load.start()

    for small, big in ((w1, big1), (w2, big2)):
        for i in range(4):
            for j in range(3):
                at = (i * 3 + j) * ch
                big[at : at + ch, 0:ch] = small[i, j] if i < 3 else jnp.zeros((ch, ch), BF16)
                big[at : at + ch, ch : 2 * ch] = small[i - 1, j] if i > 0 else jnp.zeros((ch, ch), BF16)

    def first_refs(s, d):
        dr, dq = DIRS[d]
        dst_k = {-1: pl.ds(pairs + 2, 2), 0: pl.ds(2, pairs), 1: pl.ds(0, 2)}[dr]
        src_k = {-1: pl.ds(0, 2), 0: pl.ds(0, pairs), 1: pl.ds(pairs - 2, 2)}[dr]
        if dq == 0:
            return raster.at[s, src_k], xp1.at[s, dst_k, :, pl.ds(PAD, cols), :]
        side = 1 if dq == 1 else 0
        return p_edge.at[s, side, src_k], p_land.at[s, 1 - side, dst_k]

    def second_refs(s, d):
        dr, dq = DIRS[d]
        dst_r = {-1: pl.ds(rows + 8, 8), 0: pl.ds(8, rows), 1: pl.ds(0, 8)}[dr]
        src_r = {-1: pl.ds(0, 8), 0: pl.ds(0, rows), 1: pl.ds(rows - 8, 8)}[dr]
        if dq == 0:
            src_p = {-1: pl.ds(8, 8), 1: pl.ds(rows, 8)}[dr]
            return xp2.at[s, src_p, pl.ds(PAD, cols), :], xp2.at[s, dst_r, pl.ds(PAD, cols), :]
        side = 1 if dq == 1 else 0
        return q_edge.at[s, side, src_r], q_land.at[s, 1 - side, dst_r]

    def halo(phase, s, d):
        src, dst = (first_refs, second_refs)[phase](s, d)
        dr, dq = DIRS[d]
        return pltpu.make_async_remote_copy(
            src_ref=src, dst_ref=dst,
            send_sem=h_send.at[phase, s, d], recv_sem=h_recv.at[phase, s, d],
            device_id=place(r + dr, q + dq), device_id_type=MESH,
        )

    def start_halo(phase, s):
        for d in (3, 2, 0, 1, 4, 5, 6, 7):
            dr, dq = DIRS[d]

            @pl.when(exists(r + dr, q + dq))
            def _(d=d):
                halo(phase, s, d).start()

    def zero_halo(phase, s):
        for d in range(8):
            dr, dq = DIRS[d]

            @pl.when(jnp.logical_not(exists(r - dr, q - dq)))
            def _(d=d):
                dst = (first_refs, second_refs)[phase](s, d)[1]
                dst[...] = jnp.zeros(dst.shape, BF16)

    def recv_halo(phase, s):
        for d in range(8):
            dr, dq = DIRS[d]

            @pl.when(exists(r - dr, q - dq))
            def _(d=d):
                halo(phase, s, d).wait_recv()

    def sent_halo(phase, s):
        for d in range(8):
            dr, dq = DIRS[d]

            @pl.when(exists(r + dr, q + dq))
            def _(d=d):
                halo(phase, s, d).wait_send()

    for phase in range(2):
        for s in range(scenes):
            zero_halo(phase, s)

    def pack(s):
        @pl.loop(0, pairs // 8)
        def _(t):
            at = pl.ds(2 + t * 8, 8)
            to = pl.ds(t * 8, 8)
            for side, col in ((0, PAD), (1, PAD + cols - 4)):
                for par in range(2):
                    p_edge[s, side, to, 4 * par : 4 * par + 4, :] = xp1[s, at, par, col : col + 4, :]

    loads[0].wait()
    pack(0)
    count = jnp.int32(nr - 1 + nq - 1)
    for dr, dq in DIRS[4:]:
        count = count + exists(r + dr, q + dq).astype(jnp.int32)
    pl.semaphore_wait(barrier, count)
    start_halo(0, 0)

    here = queries.shape[0]

    def key_copy(d):
        other = (a + d) % na
        return pltpu.make_async_remote_copy(
            src_ref=queries, dst_ref=everyone.at[a],
            send_sem=k_send.at[d], recv_sem=k_recv.at[d],
            device_id=place(r, c * na + other), device_id_type=MESH,
        )

    for d in range(1, na):
        key_copy(d).start()
    everyone[a] = queries[...]

    for s in range(1, scenes):
        loads[s].wait()
        pack(s)
        start_halo(0, s)

    for d in range(1, na):
        key_copy(d).wait()
    table = everyone[...].reshape(na * here, ch)
    pick = (lax.broadcasted_iota(jnp.int32, (agents, agents), 0) == slot[...]).astype(F32).astype(BF16)
    keys = lax.dot_general(
        table, pick, (((0,), (0,)), ((), ())), preferred_element_type=F32
    ).astype(BF16)
    keys_out[...] = keys

    bias1 = jnp.concatenate([b1[...], b1[...]], axis=1)
    bias2 = jnp.concatenate([b2[...], b2[...]], axis=1)

    def layer_one(s):
        recv_halo(0, s)
        for k0 in range(0, pairs + 4, 4):
            for par in range(2):
                xp1[s, k0 : k0 + 4, par, PAD - 4 : PAD, :] = p_land[s, 0, k0 : k0 + 4, 4 * par : 4 * par + 4, :]
                xp1[s, k0 : k0 + 4, par, PAD + cols : PAD + cols + 4, :] = (
                    p_land[s, 1, k0 : k0 + 4, 4 * par : 4 * par + 4, :]
                )

        @pl.loop(0, rows // 16)
        def _(g):
            def piece(i, j):
                parts = [
                    xp1[s, pl.ds(8 * g + 4 * h + 2 * i, 2), :, PAD - 4 + 4 * j : PAD - 4 + 4 * j + cols, :]
                    .reshape(4 * cols, ch)
                    for h in range(2)
                ]
                return jnp.concatenate(parts, axis=0)

            lhs = jnp.concatenate([piece(i, j) for i in range(4) for j in range(3)], axis=1)
            out = jnp.dot(lhs, big1[...], preferred_element_type=F32)
            out = jnp.maximum(out + bias1, 0.0).astype(BF16)
            for h in range(2):
                for o in range(2):
                    y = out[h * 4 * cols : (h + 1) * 4 * cols, o * ch : (o + 1) * ch].reshape(4, cols, ch)
                    at = 16 * g + 8 * h + 4 * o
                    xp2[s, pl.ds(8 + at, 4), PAD : PAD + cols, :] = y
                    q_edge[s, 0, pl.ds(at, 4)] = y[:, 0:8]
                    q_edge[s, 1, pl.ds(at, 4)] = y[:, cols - 8 : cols]

        start_halo(1, s)

    def layer_two(s):
        recv_halo(1, s)
        for k0 in range(0, rows + 16, 16):
            xp2[s, k0 : k0 + 16, PAD - 8 : PAD, :] = q_land[s, 0, k0 : k0 + 16]
            xp2[s, k0 : k0 + 16, PAD + cols : PAD + cols + 8, :] = q_land[s, 1, k0 : k0 + 16]

        peak = jnp.full((1, agents), NEG, F32)
        mass = jnp.zeros((1, agents), F32)
        for block in range(rows // BLOCK):
            def step(t, carry):
                top, total = carry
                g = block * (BLOCK // 16) + t

                def piece(i, j):
                    return xp2[
                        s, pl.ds(16 * g + 8 * i, 8), PAD - 8 + 8 * j : PAD - 8 + 8 * j + cols, :
                    ].reshape(8 * cols, ch)

                lhs = jnp.concatenate([piece(i, j) for i in range(4) for j in range(3)], axis=1)
                out = jnp.dot(lhs, big2[...], preferred_element_type=F32)
                out = jnp.maximum(out + bias2, 0.0).astype(BF16)
                for o in range(2):
                    y = out[:, o * ch : (o + 1) * ch]
                    l2[s, pl.ds(16 * g + 8 * o, 8)] = y.reshape(8, cols, ch)
                    z = jnp.dot(y, keys_out[...], preferred_element_type=F32).reshape(cols, 8, agents)
                    new = jnp.maximum(top, jnp.max(z, axis=0))
                    total = total * jnp.exp(top - new) + jnp.sum(jnp.exp(z - new[None]), axis=0)
                    top = new
                return top, total

            top, total = lax.fori_loop(
                0, BLOCK // 16, step,
                (jnp.full((8, agents), NEG, F32), jnp.zeros((8, agents), F32)),
            )
            high = jnp.max(top, axis=0, keepdims=True)
            part = jnp.sum(total * jnp.exp(top - high), axis=0, keepdims=True)
            block_row = r * (rows // BLOCK) + block
            block_col = q * cols // BLOCK
            ok = (
                (regions[0:1] <= block_row) & (block_row < regions[1:2])
                & (regions[2:3] <= block_col) & (block_col < regions[3:4])
            )
            high = jnp.where(ok, high, NEG)
            part = jnp.where(ok, part, 0.0)
            new = jnp.maximum(peak, high)
            mass = mass * jnp.exp(peak - new) + part * jnp.exp(high - new)
            peak = new
        return peak, mass

    for s in range(scenes):
        layer_one(s)
    peaks, masses = [], []
    outs = []
    for s in range(scenes):
        peak, mass = layer_two(s)
        peaks.append(peak)
        masses.append(mass)
        out = pltpu.make_async_copy(l2.at[s], l2_out.at[s], out_sem.at[s])
        out.start()
        outs.append(out)

    def stat_copy(src, got, send, recv, me, rr, qq, d):
        return pltpu.make_async_remote_copy(
            src_ref=src, dst_ref=got.at[d], send_sem=send.at[d], recv_sem=recv.at[d],
            device_id=place(rr, qq), device_id_type=MESH,
        )

    def merge(tops, parts):
        top = functools.reduce(jnp.maximum, tops)
        return top, functools.reduce(jnp.add, [p * jnp.exp(t - top) for t, p in zip(tops, parts)])

    top = jnp.concatenate(peaks, axis=0)
    part = jnp.concatenate(masses, axis=0)
    for stage, (size, got, send, recv) in enumerate(
        ((nq, got_q, sq_send, sq_recv), (nr, got_r, sr_send, sr_recv))
    ):
        mine[stage, 0] = top
        mine[stage, 1] = part
        copies = []
        for d in range(1, size):
            rr, qq = (r, (q + d) % nq) if stage == 0 else ((r + d) % nr, q)
            copies.append(stat_copy(mine.at[stage], got, send, recv, None, rr, qq, d))
            copies[-1].start()
        for copy in copies:
            copy.wait()
        top, part = merge(
            [top] + [got[d, 0] for d in range(1, size)],
            [part] + [got[d, 1] for d in range(1, size)],
        )
    norm_out[...] = top + jnp.log(part)

    for phase in range(2):
        for s in range(scenes):
            sent_halo(phase, s)
    for out in outs:
        out.wait()


def heat_kernel(field, keys, norm, out):
    out[0] = jnp.dot(field[0], keys[...], preferred_element_type=F32) - norm[0]


def shards(nr, nc, na, raster, w1, b1, w2, b2, queries, slot, regions):
    scenes, rows, cols, ch = raster.shape
    agents = slot.shape[0]
    nq = nc * na
    vmem = pl.BlockSpec(memory_space=pltpu.VMEM)
    anywhere = pl.BlockSpec(memory_space=pl.ANY)
    dma = pltpu.SemaphoreType.DMA
    field, keys, norm = pl.pallas_call(
        functools.partial(field_kernel, nr, nc, na, scenes, rows, cols, agents),
        out_shape=(
            jax.ShapeDtypeStruct((scenes, rows, cols, ch), BF16),
            jax.ShapeDtypeStruct((ch, agents), BF16),
            jax.ShapeDtypeStruct((scenes, agents), F32),
        ),
        in_specs=[anywhere] + [vmem] * 7,
        out_specs=(anywhere, vmem, vmem),
        scratch_shapes=[
            pltpu.VMEM((scenes, rows // 2 + 4, 2, cols + 2 * PAD, ch), BF16),
            pltpu.VMEM((scenes, rows + 16, cols + 2 * PAD, ch), BF16),
            pltpu.VMEM((scenes, rows, cols, ch), BF16),
            pltpu.VMEM((scenes, 2, rows // 2, 8, ch), BF16),
            pltpu.VMEM((scenes, 2, rows // 2 + 4, 8, ch), BF16),
            pltpu.VMEM((scenes, 2, rows, 8, ch), BF16),
            pltpu.VMEM((scenes, 2, rows + 16, 8, ch), BF16),
            pltpu.VMEM((12 * ch, 2 * ch), BF16),
            pltpu.VMEM((12 * ch, 2 * ch), BF16),
            pltpu.VMEM((na,) + queries.shape, BF16),
            pltpu.VMEM((2, 2, scenes, agents), F32),
            pltpu.VMEM((nq, 2, scenes, agents), F32),
            pltpu.VMEM((nr, 2, scenes, agents), F32),
            dma((scenes,)),
            dma((scenes,)),
            dma((2, scenes, 8)),
            dma((2, scenes, 8)),
            dma((na,)),
            dma((na,)),
            dma((nq,)),
            dma((nq,)),
            dma((nr,)),
            dma((nr,)),
        ],
        compiler_params=pltpu.CompilerParams(
            collective_id=0, has_side_effects=True, vmem_limit_bytes=60 * 1024 * 1024
        ),
        name="field",
    )(
        raster.reshape(scenes, rows // 2, 2, cols, ch), w1, b1.reshape(1, -1), w2, b2.reshape(1, -1),
        queries, slot.reshape(1, -1), regions.T,
    )
    cells = rows * cols
    step = min(2048, cells)
    heat = pl.pallas_call(
        heat_kernel,
        grid=(scenes, cells // step),
        out_shape=jax.ShapeDtypeStruct((scenes, cells, agents), F32),
        in_specs=[
            pl.BlockSpec((1, step, ch), lambda s, t: (s, t, 0)),
            pl.BlockSpec((ch, agents), lambda s, t: (0, 0)),
            pl.BlockSpec((1, 1, agents), lambda s, t: (s, 0, 0)),
        ],
        out_specs=pl.BlockSpec((1, step, agents), lambda s, t: (s, t, 0)),
        name="heat",
    )(field.reshape(scenes, cells, ch), keys, norm.reshape(scenes, 1, agents))
    return heat.reshape(scenes, rows, cols, agents)


def solution(mesh):
    in_specs = (P(None, "row", ("col", "agent"), None), P(), P(), P(), P(), P("agent", None), P(), P())
    out_specs = P(None, "row", ("col", "agent"), None)
    sizes = (mesh.shape["row"], mesh.shape["col"], mesh.shape["agent"])
    return jax.shard_map(
        functools.partial(shards, *sizes), mesh=mesh, in_specs=in_specs, out_specs=out_specs, check_vma=False
    )
```

```python
import functools

import jax
import jax.numpy as jnp
from jax import lax
from jax.experimental import pallas as pl
from jax.experimental.pallas import tpu as pltpu
from jax.sharding import PartitionSpec as P

BLOCK = 64
PAD = 16
NEG = -1e30
MESH = pl.DeviceIdType.MESH
DIRS = ((-1, 0), (1, 0), (0, -1), (0, 1), (-1, -1), (-1, 1), (1, -1), (1, 1))
BF16 = jnp.bfloat16
F32 = jnp.float32


def field_kernel(
    nr, nc, na, scenes, rows, cols, agents,
    raster, w1, b1, w2, b2, queries, slot, regions,
    l2_out, keys_out, norm_out,
    xp1, xp2, l2, z_ref, tops, sums, p_edge, p_land, q_edge, q_land, big1, big2, everyone,
    mine, got_q, got_r,
    load_sem, out_sem, h_send, h_recv, k_send, k_recv, sq_send, sq_recv, sr_send, sr_recv,
):
    r = lax.axis_index("row")
    c = lax.axis_index("col")
    a = lax.axis_index("agent")
    nq = nc * na
    q = c * na + a
    pairs = rows // 2
    ch = w1.shape[-1]

    def place(rr, qq):
        return {"row": rr, "col": qq // na, "agent": qq % na}

    def exists(rr, qq):
        return (rr >= 0) & (rr < nr) & (qq >= 0) & (qq < nq)

    barrier = pltpu.get_barrier_semaphore()
    for d in range(1, nr):
        pl.semaphore_signal(barrier, inc=1, device_id=place((r + d) % nr, q), device_id_type=MESH)
    for d in range(1, nq):
        pl.semaphore_signal(barrier, inc=1, device_id=place(r, (q + d) % nq), device_id_type=MESH)
    for dr, dq in DIRS[4:]:
        @pl.when(exists(r + dr, q + dq))
        def _(dr=dr, dq=dq):
            pl.semaphore_signal(barrier, inc=1, device_id=place(r + dr, q + dq), device_id_type=MESH)

    loads = [
        pltpu.make_async_copy(
            raster.at[s], xp1.at[s, pl.ds(2, pairs), :, pl.ds(PAD, cols), :], load_sem.at[s]
        )
        for s in range(scenes)
    ]
    for load in loads:
        load.start()

    for small, big in ((w1, big1), (w2, big2)):
        for i in range(4):
            for j in range(3):
                at = (i * 3 + j) * ch
                big[at : at + ch, 0:ch] = small[i, j] if i < 3 else jnp.zeros((ch, ch), BF16)
                big[at : at + ch, ch : 2 * ch] = small[i - 1, j] if i > 0 else jnp.zeros((ch, ch), BF16)

    def first_refs(s, d):
        dr, dq = DIRS[d]
        dst_k = {-1: pl.ds(pairs + 2, 2), 0: pl.ds(2, pairs), 1: pl.ds(0, 2)}[dr]
        src_k = {-1: pl.ds(0, 2), 0: pl.ds(0, pairs), 1: pl.ds(pairs - 2, 2)}[dr]
        if dq == 0:
            return raster.at[s, src_k], xp1.at[s, dst_k, :, pl.ds(PAD, cols), :]
        side = 1 if dq == 1 else 0
        return p_edge.at[s, side, src_k], p_land.at[s, 1 - side, dst_k]

    def second_refs(s, d):
        dr, dq = DIRS[d]
        dst_r = {-1: pl.ds(rows + 8, 8), 0: pl.ds(8, rows), 1: pl.ds(0, 8)}[dr]
        src_r = {-1: pl.ds(0, 8), 0: pl.ds(0, rows), 1: pl.ds(rows - 8, 8)}[dr]
        if dq == 0:
            src_p = {-1: pl.ds(8, 8), 1: pl.ds(rows, 8)}[dr]
            return xp2.at[s, src_p, pl.ds(PAD, cols), :], xp2.at[s, dst_r, pl.ds(PAD, cols), :]
        side = 1 if dq == 1 else 0
        return q_edge.at[s, side, src_r], q_land.at[s, 1 - side, dst_r]

    def halo(phase, s, d):
        src, dst = (first_refs, second_refs)[phase](s, d)
        dr, dq = DIRS[d]
        return pltpu.make_async_remote_copy(
            src_ref=src, dst_ref=dst,
            send_sem=h_send.at[phase, s, d], recv_sem=h_recv.at[phase, s, d],
            device_id=place(r + dr, q + dq), device_id_type=MESH,
        )

    def start_halo(phase, s):
        for d in (3, 2, 0, 1, 4, 5, 6, 7):
            dr, dq = DIRS[d]

            @pl.when(exists(r + dr, q + dq))
            def _(d=d):
                halo(phase, s, d).start()

    def zero_halo(phase, s):
        for d in range(8):
            dr, dq = DIRS[d]

            @pl.when(jnp.logical_not(exists(r - dr, q - dq)))
            def _(d=d):
                dst = (first_refs, second_refs)[phase](s, d)[1]
                dst[...] = jnp.zeros(dst.shape, BF16)

    def recv_halo(phase, s):
        for d in range(8):
            dr, dq = DIRS[d]

            @pl.when(exists(r - dr, q - dq))
            def _(d=d):
                halo(phase, s, d).wait_recv()

    def sent_halo(phase, s):
        for d in range(8):
            dr, dq = DIRS[d]

            @pl.when(exists(r + dr, q + dq))
            def _(d=d):
                halo(phase, s, d).wait_send()

    for phase in range(2):
        for s in range(scenes):
            zero_halo(phase, s)

    def pack(s):
        @pl.loop(0, pairs // 8)
        def _(t):
            at = pl.ds(2 + t * 8, 8)
            to = pl.ds(t * 8, 8)
            for side, col in ((0, PAD), (1, PAD + cols - 4)):
                for par in range(2):
                    p_edge[s, side, to, 4 * par : 4 * par + 4, :] = xp1[s, at, par, col : col + 4, :]

    loads[0].wait()
    pack(0)
    count = jnp.int32(nr - 1 + nq - 1)
    for dr, dq in DIRS[4:]:
        count = count + exists(r + dr, q + dq).astype(jnp.int32)
    pl.semaphore_wait(barrier, count)
    start_halo(0, 0)

    here = queries.shape[0]

    def key_copy(d):
        other = (a + d) % na
        return pltpu.make_async_remote_copy(
            src_ref=queries, dst_ref=everyone.at[a],
            send_sem=k_send.at[d], recv_sem=k_recv.at[d],
            device_id=place(r, c * na + other), device_id_type=MESH,
        )

    for d in range(1, na):
        key_copy(d).start()
    everyone[a] = queries[...]

    for s in range(1, scenes):
        loads[s].wait()
        pack(s)
        start_halo(0, s)

    for d in range(1, na):
        key_copy(d).wait()
    table = everyone[...].reshape(na * here, ch)
    pick = (lax.broadcasted_iota(jnp.int32, (agents, agents), 0) == slot[...]).astype(F32).astype(BF16)
    keys = lax.dot_general(
        table, pick, (((0,), (0,)), ((), ())), preferred_element_type=F32
    ).astype(BF16)
    keys_out[...] = keys

    bias1 = jnp.concatenate([b1[...], b1[...]], axis=1)
    bias2 = jnp.concatenate([b2[...], b2[...]], axis=1)

    def layer_one(s):
        recv_halo(0, s)
        for k0 in range(0, pairs + 4, 4):
            for par in range(2):
                xp1[s, k0 : k0 + 4, par, PAD - 4 : PAD, :] = p_land[s, 0, k0 : k0 + 4, 4 * par : 4 * par + 4, :]
                xp1[s, k0 : k0 + 4, par, PAD + cols : PAD + cols + 4, :] = (
                    p_land[s, 1, k0 : k0 + 4, 4 * par : 4 * par + 4, :]
                )

        @pl.loop(0, rows // 16)
        def _(g):
            def piece(i, j):
                parts = [
                    xp1[s, pl.ds(8 * g + 4 * h + 2 * i, 2), :, PAD - 4 + 4 * j : PAD - 4 + 4 * j + cols, :]
                    .reshape(4 * cols, ch)
                    for h in range(2)
                ]
                return jnp.concatenate(parts, axis=0)

            lhs = jnp.concatenate([piece(i, j) for i in range(4) for j in range(3)], axis=1)
            out = jnp.dot(lhs, big1[...], preferred_element_type=F32)
            out = jnp.maximum(out + bias1, 0.0).astype(BF16)
            for h in range(2):
                for o in range(2):
                    y = out[h * 4 * cols : (h + 1) * 4 * cols, o * ch : (o + 1) * ch].reshape(4, cols, ch)
                    at = 16 * g + 8 * h + 4 * o
                    xp2[s, pl.ds(8 + at, 4), PAD : PAD + cols, :] = y
                    q_edge[s, 0, pl.ds(at, 4)] = y[:, 0:8]
                    q_edge[s, 1, pl.ds(at, 4)] = y[:, cols - 8 : cols]

        start_halo(1, s)

    def layer_two(s):
        recv_halo(1, s)
        for k0 in range(0, rows + 16, 16):
            xp2[s, k0 : k0 + 16, PAD - 8 : PAD, :] = q_land[s, 0, k0 : k0 + 16]
            xp2[s, k0 : k0 + 16, PAD + cols : PAD + cols + 8, :] = q_land[s, 1, k0 : k0 + 16]

        @pl.loop(0, steps)
        def _(t):
            fold(s * steps + t - 2)
            score(s * steps + t - 1)

            def piece(i, j):
                return xp2[
                    s, pl.ds(16 * t + 8 * i, 8), PAD - 8 + 8 * j : PAD - 8 + 8 * j + cols, :
                ].reshape(8 * cols, ch)

            lhs = jnp.concatenate([piece(i, j) for i in range(4) for j in range(3)], axis=1)
            out = jnp.dot(lhs, big2[...], preferred_element_type=F32)
            out = jnp.maximum(out + bias2, 0.0).astype(BF16)
            for o in range(2):
                at = s * rows + 16 * t + 8 * o
                l2[pl.ds(at, 8)] = out[:, o * ch : (o + 1) * ch].reshape(8, cols, ch)

    def settle(s):
        peak = jnp.full((1, agents), NEG, F32)
        mass = jnp.zeros((1, agents), F32)
        for block in range(rows // BLOCK):
            top = tops[s * (rows // BLOCK) + block]
            total = sums[s * (rows // BLOCK) + block]
            high = jnp.max(top, axis=0, keepdims=True)
            part = jnp.sum(total * jnp.exp(top - high), axis=0, keepdims=True)
            block_row = r * (rows // BLOCK) + block
            block_col = q * cols // BLOCK
            ok = (
                (regions[0:1] <= block_row) & (block_row < regions[1:2])
                & (regions[2:3] <= block_col) & (block_col < regions[3:4])
            )
            high = jnp.where(ok, high, NEG)
            part = jnp.where(ok, part, 0.0)
            new = jnp.maximum(peak, high)
            mass = mass * jnp.exp(peak - new) + part * jnp.exp(high - new)
            peak = new
        return peak, mass

    steps = rows // 16
    spare = scenes * rows // BLOCK

    def score(u):
        at = 16 * jnp.maximum(u, 0) if not isinstance(u, int) else 16 * u
        y = l2[pl.ds(at, 16)].reshape(16 * cols, ch)
        z_ref[...] = jnp.dot(y, keys_out[...], preferred_element_type=F32)

    def fold(u):
        slot = u // (BLOCK // 16) if isinstance(u, int) else jnp.where(u >= 0, u // (BLOCK // 16), spare)
        top, total = tops[slot], sums[slot]
        size = 64
        chunks = 16 * cols // size
        maxes = [top]
        for k in range(chunks):
            m = jnp.max(z_ref[k * size : (k + 1) * size].reshape(size // 8, 8, agents), axis=0)
            if k < 4:
                maxes.append(m)
            else:
                maxes[1 + k % 4] = jnp.maximum(maxes[1 + k % 4], m)
        new = functools.reduce(jnp.maximum, maxes)
        total = total * jnp.exp(top - new)
        for k in range(chunks):
            z = z_ref[k * size : (k + 1) * size].reshape(size // 8, 8, agents)
            total = total + jnp.sum(jnp.exp(z - new[None]), axis=0)
        tops[slot] = new
        sums[slot] = total

    z_ref[...] = jnp.zeros(z_ref.shape, F32)
    l2[0:16] = jnp.zeros((16, cols, ch), BF16)
    tops[...] = jnp.full(tops.shape, NEG, F32)
    sums[...] = jnp.zeros(sums.shape, F32)

    for s in range(scenes):
        layer_one(s)
    peaks, masses = [], []
    outs = []
    for s in range(scenes):
        layer_two(s)
        if s == scenes - 1:
            fold(scenes * steps - 2)
            score(scenes * steps - 1)
            fold(scenes * steps - 1)
        out = pltpu.make_async_copy(l2.at[pl.ds(s * rows, rows)], l2_out.at[s], out_sem.at[s])
        out.start()
        outs.append(out)
    for s in range(scenes):
        peak, mass = settle(s)
        peaks.append(peak)
        masses.append(mass)

    def stat_copy(src, got, send, recv, me, rr, qq, d):
        return pltpu.make_async_remote_copy(
            src_ref=src, dst_ref=got.at[d], send_sem=send.at[d], recv_sem=recv.at[d],
            device_id=place(rr, qq), device_id_type=MESH,
        )

    def merge(tops, parts):
        top = functools.reduce(jnp.maximum, tops)
        return top, functools.reduce(jnp.add, [p * jnp.exp(t - top) for t, p in zip(tops, parts)])

    top = jnp.concatenate(peaks, axis=0)
    part = jnp.concatenate(masses, axis=0)
    for stage, (size, got, send, recv) in enumerate(
        ((nq, got_q, sq_send, sq_recv), (nr, got_r, sr_send, sr_recv))
    ):
        mine[stage, 0] = top
        mine[stage, 1] = part
        copies = []
        for d in range(1, size):
            rr, qq = (r, (q + d) % nq) if stage == 0 else ((r + d) % nr, q)
            copies.append(stat_copy(mine.at[stage], got, send, recv, None, rr, qq, d))
            copies[-1].start()
        for copy in copies:
            copy.wait()
        top, part = merge(
            [top] + [got[d, 0] for d in range(1, size)],
            [part] + [got[d, 1] for d in range(1, size)],
        )
    norm_out[...] = top + jnp.log(part)

    for phase in range(2):
        for s in range(scenes):
            sent_halo(phase, s)
    for out in outs:
        out.wait()


def heat_kernel(field, keys, norm, out, cells, heat, in_sem, out_sem):
    scenes, total, _ = field.shape
    parts, size = cells.shape[0], cells.shape[1]
    slots = heat.shape[0]
    per = total // size
    loads = []
    for t in range(parts):
        load = pltpu.make_async_copy(
            field.at[t // per, pl.ds(t % per * size, size)], cells.at[t], in_sem.at[t]
        )
        load.start()
        loads.append(load)
    stores = []
    for t in range(parts):
        if t >= slots:
            stores[t - slots].wait()
        loads[t].wait()
        s = t // per
        heat[t % slots] = jnp.dot(cells[t], keys[...], preferred_element_type=F32) - norm[s : s + 1]
        store = pltpu.make_async_copy(
            heat.at[t % slots], out.at[s, pl.ds(t % per * size, size)], out_sem.at[t % slots]
        )
        store.start()
        stores.append(store)
    for store in stores[max(parts - slots, 0):]:
        store.wait()


def shards(nr, nc, na, raster, w1, b1, w2, b2, queries, slot, regions):
    scenes, rows, cols, ch = raster.shape
    agents = slot.shape[0]
    nq = nc * na
    vmem = pl.BlockSpec(memory_space=pltpu.VMEM)
    anywhere = pl.BlockSpec(memory_space=pl.ANY)
    dma = pltpu.SemaphoreType.DMA
    field, keys, norm = pl.pallas_call(
        functools.partial(field_kernel, nr, nc, na, scenes, rows, cols, agents),
        out_shape=(
            jax.ShapeDtypeStruct((scenes, rows, cols, ch), BF16),
            jax.ShapeDtypeStruct((ch, agents), BF16),
            jax.ShapeDtypeStruct((scenes, agents), F32),
        ),
        in_specs=[anywhere] + [vmem] * 7,
        out_specs=(anywhere, vmem, vmem),
        scratch_shapes=[
            pltpu.VMEM((scenes, rows // 2 + 4, 2, cols + 2 * PAD, ch), BF16),
            pltpu.VMEM((scenes, rows + 16, cols + 2 * PAD, ch), BF16),
            pltpu.VMEM((scenes * rows, cols, ch), BF16),
            pltpu.VMEM((16 * cols, agents), F32),
            pltpu.VMEM((scenes * rows // BLOCK + 1, 8, agents), F32),
            pltpu.VMEM((scenes * rows // BLOCK + 1, 8, agents), F32),
            pltpu.VMEM((scenes, 2, rows // 2, 8, ch), BF16),
            pltpu.VMEM((scenes, 2, rows // 2 + 4, 8, ch), BF16),
            pltpu.VMEM((scenes, 2, rows, 8, ch), BF16),
            pltpu.VMEM((scenes, 2, rows + 16, 8, ch), BF16),
            pltpu.VMEM((12 * ch, 2 * ch), BF16),
            pltpu.VMEM((12 * ch, 2 * ch), BF16),
            pltpu.VMEM((na,) + queries.shape, BF16),
            pltpu.VMEM((2, 2, scenes, agents), F32),
            pltpu.VMEM((nq, 2, scenes, agents), F32),
            pltpu.VMEM((nr, 2, scenes, agents), F32),
            dma((scenes,)),
            dma((scenes,)),
            dma((2, scenes, 8)),
            dma((2, scenes, 8)),
            dma((na,)),
            dma((na,)),
            dma((nq,)),
            dma((nq,)),
            dma((nr,)),
            dma((nr,)),
        ],
        compiler_params=pltpu.CompilerParams(
            collective_id=0, has_side_effects=True, vmem_limit_bytes=60 * 1024 * 1024
        ),
        name="field",
    )(
        raster.reshape(scenes, rows // 2, 2, cols, ch), w1, b1.reshape(1, -1), w2, b2.reshape(1, -1),
        queries, slot.reshape(1, -1), regions.T,
    )
    cells = rows * cols
    size = min(2048, cells)
    parts = scenes * cells // size
    slots = min(4, parts)
    heat = pl.pallas_call(
        heat_kernel,
        out_shape=jax.ShapeDtypeStruct((scenes, cells, agents), F32),
        in_specs=[anywhere, vmem, vmem],
        out_specs=anywhere,
        scratch_shapes=[
            pltpu.VMEM((parts, size, ch), BF16),
            pltpu.VMEM((slots, size, agents), F32),
            dma((parts,)),
            dma((slots,)),
        ],
        name="heat",
    )(field.reshape(scenes, cells, ch), keys, norm)
    return heat.reshape(scenes, rows, cols, agents)


def solution(mesh):
    in_specs = (P(None, "row", ("col", "agent"), None), P(), P(), P(), P(), P("agent", None), P(), P())
    out_specs = P(None, "row", ("col", "agent"), None)
    sizes = (mesh.shape["row"], mesh.shape["col"], mesh.shape["agent"])
    return jax.shard_map(
        functools.partial(shards, *sizes), mesh=mesh, in_specs=in_specs, out_specs=out_specs, check_vma=False
    )
```

```python
import functools

import jax
import jax.numpy as jnp
from jax import lax
from jax.experimental import pallas as pl
from jax.experimental.pallas import tpu as pltpu
from jax.sharding import PartitionSpec as P

BLOCK = 64
PAD = 16
NEG = -1e30
MESH = pl.DeviceIdType.MESH
DIRS = ((-1, 0), (1, 0), (0, -1), (0, 1), (-1, -1), (-1, 1), (1, -1), (1, 1))
FIRST = (3, 2, 0, 1, 4, 5, 6, 7, 9, 8)
PIECES = DIRS + ((0, -1), (0, 1))
BF16 = jnp.bfloat16
F32 = jnp.float32


def field_kernel(
    nr, nc, na, scenes, rows, cols, agents,
    raster, w1, b1, w2, b2, queries, slot, regions,
    l2_out, keys_out, norm_out,
    xp1, xp2, l2, z_ref, tops, sums, p_edge, p_land, q_edge, q_land, big1, big2, everyone,
    mine, got_q, got_r,
    load_sem, out_sem, h_send, h_recv, k_send, k_recv, sq_send, sq_recv, sr_send, sr_recv,
):
    r = lax.axis_index("row")
    c = lax.axis_index("col")
    a = lax.axis_index("agent")
    nq = nc * na
    q = c * na + a
    pairs = rows // 2
    ch = w1.shape[-1]
    cut1 = pairs // 2 + 2

    def place(rr, qq):
        return {"row": rr, "col": qq // na, "agent": qq % na}

    def exists(rr, qq):
        return (rr >= 0) & (rr < nr) & (qq >= 0) & (qq < nq)

    barrier = pltpu.get_barrier_semaphore()
    for d in range(1, nr):
        pl.semaphore_signal(barrier, inc=1, device_id=place((r + d) % nr, q), device_id_type=MESH)
    for d in range(1, nq):
        pl.semaphore_signal(barrier, inc=1, device_id=place(r, (q + d) % nq), device_id_type=MESH)
    for dr, dq in DIRS[4:]:
        @pl.when(exists(r + dr, q + dq))
        def _(dr=dr, dq=dq):
            pl.semaphore_signal(barrier, inc=1, device_id=place(r + dr, q + dq), device_id_type=MESH)

    loads = [
        pltpu.make_async_copy(
            raster.at[s], xp1.at[s, pl.ds(2, pairs), :, pl.ds(PAD, cols), :], load_sem.at[s]
        )
        for s in range(scenes)
    ]
    for load in loads:
        load.start()

    for small, big in ((w1, big1), (w2, big2)):
        for i in range(4):
            for j in range(3):
                at = (i * 3 + j) * ch
                big[at : at + ch, 0:ch] = small[i, j] if i < 3 else jnp.zeros((ch, ch), BF16)
                big[at : at + ch, ch : 2 * ch] = small[i - 1, j] if i > 0 else jnp.zeros((ch, ch), BF16)

    def first_refs(s, d):
        dr, dq = PIECES[d]
        low, high = (cut1, pairs) if d >= 8 else (0, cut1)
        dst_k = {-1: pl.ds(pairs + 2, 2), 0: pl.ds(2 + low, high - low), 1: pl.ds(0, 2)}[dr]
        src_k = {-1: pl.ds(0, 2), 0: pl.ds(low, high - low), 1: pl.ds(pairs - 2, 2)}[dr]
        if dq == 0:
            return raster.at[s, src_k], xp1.at[s, dst_k, :, pl.ds(PAD, cols), :]
        side = 1 if dq == 1 else 0
        return p_edge.at[s, side, src_k], p_land.at[s, 1 - side, dst_k]

    def second_refs(s, d):
        dr, dq = PIECES[d]
        low, high = (rows // 2, rows) if d >= 8 else (0, rows // 2)
        dst_r = {-1: pl.ds(rows + 8, 8), 0: pl.ds(8 + low, high - low), 1: pl.ds(0, 8)}[dr]
        src_r = {-1: pl.ds(0, 8), 0: pl.ds(low, high - low), 1: pl.ds(rows - 8, 8)}[dr]
        if dq == 0:
            src_p = {-1: pl.ds(8, 8), 1: pl.ds(rows, 8)}[dr]
            return xp2.at[s, src_p, pl.ds(PAD, cols), :], xp2.at[s, dst_r, pl.ds(PAD, cols), :]
        side = 1 if dq == 1 else 0
        return q_edge.at[s, side, src_r], q_land.at[s, 1 - side, dst_r]

    def halo(phase, s, d):
        src, dst = (first_refs, second_refs)[phase](s, d)
        dr, dq = PIECES[d]
        return pltpu.make_async_remote_copy(
            src_ref=src, dst_ref=dst,
            send_sem=h_send.at[phase, s, d], recv_sem=h_recv.at[phase, s, d],
            device_id=place(r + dr, q + dq), device_id_type=MESH,
        )

    def start_halo(phase, s, picked):
        for d in picked:
            dr, dq = PIECES[d]

            @pl.when(exists(r + dr, q + dq))
            def _(d=d):
                halo(phase, s, d).start()

    def zero_halo(phase, s):
        for d in range(10):
            dr, dq = PIECES[d]

            @pl.when(jnp.logical_not(exists(r - dr, q - dq)))
            def _(d=d):
                dst = (first_refs, second_refs)[phase](s, d)[1]
                dst[...] = jnp.zeros(dst.shape, BF16)

    def recv_halo(phase, s, picked):
        for d in picked:
            dr, dq = PIECES[d]

            @pl.when(exists(r - dr, q - dq))
            def _(d=d):
                halo(phase, s, d).wait_recv()

    def sent_halo(phase, s):
        for d in range(10):
            dr, dq = PIECES[d]

            @pl.when(exists(r + dr, q + dq))
            def _(d=d):
                halo(phase, s, d).wait_send()

    for phase in range(2):
        for s in range(scenes):
            zero_halo(phase, s)

    def pack(s):
        @pl.loop(0, pairs // 8)
        def _(t):
            at = pl.ds(2 + t * 8, 8)
            to = pl.ds(t * 8, 8)
            for side, col in ((0, PAD), (1, PAD + cols - 4)):
                for par in range(2):
                    p_edge[s, side, to, 4 * par : 4 * par + 4, :] = xp1[s, at, par, col : col + 4, :]

    loads[0].wait()
    pack(0)
    count = jnp.int32(nr - 1 + nq - 1)
    for dr, dq in DIRS[4:]:
        count = count + exists(r + dr, q + dq).astype(jnp.int32)
    pl.semaphore_wait(barrier, count)
    start_halo(0, 0, FIRST)

    here = queries.shape[0]

    def key_copy(d):
        other = (a + d) % na
        return pltpu.make_async_remote_copy(
            src_ref=queries, dst_ref=everyone.at[a],
            send_sem=k_send.at[d], recv_sem=k_recv.at[d],
            device_id=place(r, c * na + other), device_id_type=MESH,
        )

    for d in range(1, na):
        key_copy(d).start()
    everyone[a] = queries[...]

    for s in range(1, scenes):
        loads[s].wait()
        pack(s)
        start_halo(0, s, FIRST)

    for d in range(1, na):
        key_copy(d).wait()
    table = everyone[...].reshape(na * here, ch)
    pick = (lax.broadcasted_iota(jnp.int32, (agents, agents), 0) == slot[...]).astype(F32).astype(BF16)
    keys = lax.dot_general(
        table, pick, (((0,), (0,)), ((), ())), preferred_element_type=F32
    ).astype(BF16)
    keys_out[...] = keys

    bias1 = jnp.concatenate([b1[...], b1[...]], axis=1)
    bias2 = jnp.concatenate([b2[...], b2[...]], axis=1)

    def layer_one(s):
        def unpack(low, high):
            for k0 in range(low, high, 4):
                for par in range(2):
                    for side, col in ((0, PAD - 4), (1, PAD + cols)):
                        xp1[s, k0 : k0 + 4, par, col : col + 4, :] = (
                            p_land[s, side, k0 : k0 + 4, 4 * par : 4 * par + 4, :]
                        )

        def sweep(low, high):
            pl.loop(low // 32, high // 32)(body)

        def body(g):
            def piece(i, j):
                parts = [
                    xp1[s, pl.ds(16 * g + 4 * h + 2 * i, 2), :, PAD - 4 + 4 * j : PAD - 4 + 4 * j + cols, :]
                    .reshape(4 * cols, ch)
                    for h in range(4)
                ]
                return jnp.concatenate(parts, axis=0)

            lhs = jnp.concatenate([piece(i, j) for i in range(4) for j in range(3)], axis=1)
            out = jnp.dot(lhs, big1[...], preferred_element_type=F32)
            out = jnp.maximum(out + bias1, 0.0).astype(BF16)
            for h in range(4):
                for o in range(2):
                    y = out[h * 4 * cols : (h + 1) * 4 * cols, o * ch : (o + 1) * ch].reshape(4, cols, ch)
                    at = 32 * g + 8 * h + 4 * o
                    xp2[s, pl.ds(8 + at, 4), PAD : PAD + cols, :] = y
                    q_edge[s, 0, pl.ds(at, 4)] = y[:, 0:8]
                    q_edge[s, 1, pl.ds(at, 4)] = y[:, cols - 8 : cols]

        recv_halo(0, s, range(8))
        unpack(0, cut1 + 2)
        sweep(0, rows // 2)
        start_halo(1, s, (3, 2, 0, 4, 5))
        recv_halo(0, s, (8, 9))
        unpack(cut1 + 2, pairs + 4)
        sweep(rows // 2, rows)
        start_halo(1, s, (9, 8, 1, 6, 7))

    def layer_two(s):
        recv_halo(1, s, range(10))
        for k0 in range(0, rows + 16, 16):
            xp2[s, k0 : k0 + 16, PAD - 8 : PAD, :] = q_land[s, 0, k0 : k0 + 16]
            xp2[s, k0 : k0 + 16, PAD + cols : PAD + cols + 8, :] = q_land[s, 1, k0 : k0 + 16]

        @pl.loop(0, steps)
        def _(t):
            fold(s * steps + t - 2)
            score(s * steps + t - 1)

            def piece(i, j):
                return xp2[
                    s, pl.ds(16 * t + 8 * i, 8), PAD - 8 + 8 * j : PAD - 8 + 8 * j + cols, :
                ].reshape(8 * cols, ch)

            lhs = jnp.concatenate([piece(i, j) for i in range(4) for j in range(3)], axis=1)
            out = jnp.dot(lhs, big2[...], preferred_element_type=F32)
            out = jnp.maximum(out + bias2, 0.0).astype(BF16)
            for o in range(2):
                at = s * rows + 16 * t + 8 * o
                l2[pl.ds(at, 8)] = out[:, o * ch : (o + 1) * ch].reshape(8, cols, ch)

    def settle(s):
        peak = jnp.full((1, agents), NEG, F32)
        mass = jnp.zeros((1, agents), F32)
        for block in range(rows // BLOCK):
            top = tops[s * (rows // BLOCK) + block]
            total = sums[s * (rows // BLOCK) + block]
            high = jnp.max(top, axis=0, keepdims=True)
            part = jnp.sum(total * jnp.exp(top - high), axis=0, keepdims=True)
            block_row = r * (rows // BLOCK) + block
            block_col = q * cols // BLOCK
            ok = (
                (regions[0:1] <= block_row) & (block_row < regions[1:2])
                & (regions[2:3] <= block_col) & (block_col < regions[3:4])
            )
            high = jnp.where(ok, high, NEG)
            part = jnp.where(ok, part, 0.0)
            new = jnp.maximum(peak, high)
            mass = mass * jnp.exp(peak - new) + part * jnp.exp(high - new)
            peak = new
        return peak, mass

    steps = rows // 16
    spare = scenes * rows // BLOCK

    def score(u):
        at = 16 * jnp.maximum(u, 0) if not isinstance(u, int) else 16 * u
        y = l2[pl.ds(at, 16)].reshape(16 * cols, ch)
        z_ref[...] = jnp.dot(y, keys_out[...], preferred_element_type=F32)

    def fold(u):
        slot = u // (BLOCK // 16) if isinstance(u, int) else jnp.where(u >= 0, u // (BLOCK // 16), spare)
        top, total = tops[slot], sums[slot]
        size = 64
        chunks = 16 * cols // size
        maxes = [top]
        for k in range(chunks):
            m = jnp.max(z_ref[k * size : (k + 1) * size].reshape(size // 8, 8, agents), axis=0)
            if k < 4:
                maxes.append(m)
            else:
                maxes[1 + k % 4] = jnp.maximum(maxes[1 + k % 4], m)
        new = functools.reduce(jnp.maximum, maxes)
        total = total * jnp.exp(top - new)
        for k in range(chunks):
            z = z_ref[k * size : (k + 1) * size].reshape(size // 8, 8, agents)
            total = total + jnp.sum(jnp.exp(z - new[None]), axis=0)
        tops[slot] = new
        sums[slot] = total

    z_ref[...] = jnp.zeros(z_ref.shape, F32)
    l2[0:16] = jnp.zeros((16, cols, ch), BF16)
    tops[...] = jnp.full(tops.shape, NEG, F32)
    sums[...] = jnp.zeros(sums.shape, F32)

    for s in range(scenes):
        layer_one(s)
    peaks, masses = [], []
    outs = []
    for s in range(scenes):
        layer_two(s)
        if s == scenes - 1:
            fold(scenes * steps - 2)
            score(scenes * steps - 1)
            fold(scenes * steps - 1)
        out = pltpu.make_async_copy(l2.at[pl.ds(s * rows, rows)], l2_out.at[s], out_sem.at[s])
        out.start()
        outs.append(out)
    for s in range(scenes):
        peak, mass = settle(s)
        peaks.append(peak)
        masses.append(mass)

    def stat_copy(src, got, send, recv, me, rr, qq, d):
        return pltpu.make_async_remote_copy(
            src_ref=src, dst_ref=got.at[d], send_sem=send.at[d], recv_sem=recv.at[d],
            device_id=place(rr, qq), device_id_type=MESH,
        )

    def merge(tops, parts):
        top = functools.reduce(jnp.maximum, tops)
        return top, functools.reduce(jnp.add, [p * jnp.exp(t - top) for t, p in zip(tops, parts)])

    top = jnp.concatenate(peaks, axis=0)
    part = jnp.concatenate(masses, axis=0)
    for stage, (size, got, send, recv) in enumerate(
        ((nq, got_q, sq_send, sq_recv), (nr, got_r, sr_send, sr_recv))
    ):
        mine[stage, 0] = top
        mine[stage, 1] = part
        copies = []
        for d in range(1, size):
            rr, qq = (r, (q + d) % nq) if stage == 0 else ((r + d) % nr, q)
            copies.append(stat_copy(mine.at[stage], got, send, recv, None, rr, qq, d))
            copies[-1].start()
        for copy in copies:
            copy.wait()
        top, part = merge(
            [top] + [got[d, 0] for d in range(1, size)],
            [part] + [got[d, 1] for d in range(1, size)],
        )
    norm_out[...] = top + jnp.log(part)

    for phase in range(2):
        for s in range(scenes):
            sent_halo(phase, s)
    for out in outs:
        out.wait()


def heat_kernel(field, keys, norm, out, cells, heat, in_sem, out_sem):
    scenes, total, _ = field.shape
    parts, size = cells.shape[0], cells.shape[1]
    slots = heat.shape[0]
    per = total // size
    loads = []
    for t in range(parts):
        load = pltpu.make_async_copy(
            field.at[t // per, pl.ds(t % per * size, size)], cells.at[t], in_sem.at[t]
        )
        load.start()
        loads.append(load)
    stores = []
    for t in range(parts):
        if t >= slots:
            stores[t - slots].wait()
        loads[t].wait()
        s = t // per
        heat[t % slots] = jnp.dot(cells[t], keys[...], preferred_element_type=F32) - norm[s : s + 1]
        store = pltpu.make_async_copy(
            heat.at[t % slots], out.at[s, pl.ds(t % per * size, size)], out_sem.at[t % slots]
        )
        store.start()
        stores.append(store)
    for store in stores[max(parts - slots, 0):]:
        store.wait()


def shards(nr, nc, na, raster, w1, b1, w2, b2, queries, slot, regions):
    scenes, rows, cols, ch = raster.shape
    agents = slot.shape[0]
    nq = nc * na
    vmem = pl.BlockSpec(memory_space=pltpu.VMEM)
    anywhere = pl.BlockSpec(memory_space=pl.ANY)
    dma = pltpu.SemaphoreType.DMA
    field, keys, norm = pl.pallas_call(
        functools.partial(field_kernel, nr, nc, na, scenes, rows, cols, agents),
        out_shape=(
            jax.ShapeDtypeStruct((scenes, rows, cols, ch), BF16),
            jax.ShapeDtypeStruct((ch, agents), BF16),
            jax.ShapeDtypeStruct((scenes, agents), F32),
        ),
        in_specs=[anywhere] + [vmem] * 7,
        out_specs=(anywhere, vmem, vmem),
        scratch_shapes=[
            pltpu.VMEM((scenes, rows // 2 + 4, 2, cols + 2 * PAD, ch), BF16),
            pltpu.VMEM((scenes, rows + 16, cols + 2 * PAD, ch), BF16),
            pltpu.VMEM((scenes * rows, cols, ch), BF16),
            pltpu.VMEM((16 * cols, agents), F32),
            pltpu.VMEM((scenes * rows // BLOCK + 1, 8, agents), F32),
            pltpu.VMEM((scenes * rows // BLOCK + 1, 8, agents), F32),
            pltpu.VMEM((scenes, 2, rows // 2, 8, ch), BF16),
            pltpu.VMEM((scenes, 2, rows // 2 + 4, 8, ch), BF16),
            pltpu.VMEM((scenes, 2, rows, 8, ch), BF16),
            pltpu.VMEM((scenes, 2, rows + 16, 8, ch), BF16),
            pltpu.VMEM((12 * ch, 2 * ch), BF16),
            pltpu.VMEM((12 * ch, 2 * ch), BF16),
            pltpu.VMEM((na,) + queries.shape, BF16),
            pltpu.VMEM((2, 2, scenes, agents), F32),
            pltpu.VMEM((nq, 2, scenes, agents), F32),
            pltpu.VMEM((nr, 2, scenes, agents), F32),
            dma((scenes,)),
            dma((scenes,)),
            dma((2, scenes, 10)),
            dma((2, scenes, 10)),
            dma((na,)),
            dma((na,)),
            dma((nq,)),
            dma((nq,)),
            dma((nr,)),
            dma((nr,)),
        ],
        compiler_params=pltpu.CompilerParams(
            collective_id=0, has_side_effects=True, vmem_limit_bytes=60 * 1024 * 1024
        ),
        name="field",
    )(
        raster.reshape(scenes, rows // 2, 2, cols, ch), w1, b1.reshape(1, -1), w2, b2.reshape(1, -1),
        queries, slot.reshape(1, -1), regions.T,
    )
    cells = rows * cols
    size = min(2048, cells)
    parts = scenes * cells // size
    slots = min(4, parts)
    heat = pl.pallas_call(
        heat_kernel,
        out_shape=jax.ShapeDtypeStruct((scenes, cells, agents), F32),
        in_specs=[anywhere, vmem, vmem],
        out_specs=anywhere,
        scratch_shapes=[
            pltpu.VMEM((parts, size, ch), BF16),
            pltpu.VMEM((slots, size, agents), F32),
            dma((parts,)),
            dma((slots,)),
        ],
        name="heat",
    )(field.reshape(scenes, cells, ch), keys, norm)
    return heat.reshape(scenes, rows, cols, agents)


def solution(mesh):
    in_specs = (P(None, "row", ("col", "agent"), None), P(), P(), P(), P(), P("agent", None), P(), P())
    out_specs = P(None, "row", ("col", "agent"), None)
    sizes = (mesh.shape["row"], mesh.shape["col"], mesh.shape["agent"])
    return jax.shard_map(
        functools.partial(shards, *sizes), mesh=mesh, in_specs=in_specs, out_specs=out_specs, check_vma=False
    )
```
